256 devices in a mesh: ctx: 64 (over y, z, core), tp: 4 (over x).
Axes of the slice: x: 4, y: 4, z: 8, core: 2. Of those that a mesh axis runs over, the one named last changes fastest.
Arguments:
- first_stream: bfloat16 [32768, 8192], P(('ctx', 'tp')), may hold values from -6 to 6
- second_stream: bfloat16 [32768, 8192], P(('ctx', 'tp')), may hold values from -6 to 6
- value_stream: bfloat16 [32768, 8192], P(('ctx', 'tp')), may hold values from -6 to 6
- short_filter: bfloat16 [3, 7, 512], replicated, may hold values from -2 to 2
- long_filter: bfloat16 [128, 512], replicated, may hold values from -0.5 to 0.5
- skip_gain: float32 [8192], replicated, may hold values from -3 to 3
- lengths: int32 [16], replicated, may hold values from 1 to 4096, 32768 in all
Outputs:
- mixed: bfloat16 [8192, 32768], P(('ctx', 'tp'))
The draws below stay inside these ranges and needn't reach their ends.
Inputs may be any that keep to these rules, and one draw needn't show every extreme that they name: The lengths of the 16 segments packed into the window in order; they sum to 32768.
All inputs are finite; a program needn't handle non-finite values.
Results may differ from the reference program's by a relative error of at most 0.0085.
Values may be sent and summed in bfloat16 or wider, within the bound.
A program may use at most 192 MiB of HBM per device.

```python
import math
import jax
import jax.numpy as jnp
import numpy as np
from jax import lax

D = 8192
GROUP = 16
GROUPS = 512
SHORT = 7
LONG = 128
TOKENS = 32768
NSEG = 16
SEG_MOST = 4096


def block_levels(key, shape, cuts, low, top_value):
    factor_of = 1.0
    for dim, blocks in cuts:
        heights = jax.random.uniform(jax.random.fold_in(jax.random.fold_in(key, 6), dim), (blocks,), jnp.float32, low / len(cuts), top_value / len(cuts))
        factor_of = factor_of * jnp.repeat(jnp.exp(heights), shape[dim] // blocks).reshape((-1,) + (1,) * (len(shape) - 1 - dim))
    return factor_of


def length_profile(count, total, limit, slope):
    portions = [(1 << 20) // math.isqrt(rank ** slope) + 1 for rank in range(2, count + 1)]
    surplus, holding = total - limit - (count - 1), [1] * (count - 1)
    while surplus > 0:
        free = [i for i in range(count - 1) if holding[i] < limit]
        whole, budget = sum([portions[i] for i in free]), surplus
        for i in free:
            more = min(limit - holding[i], max(1, budget * portions[i] // whole), surplus)
            holding[i] = holding[i] + more
            surplus = surplus - more
    return np.array([limit] + holding)


def ragged(stream_key, number_of, total, limit, lean):
    if number_of == 2:
        one = jax.random.randint(stream_key, (), max(1, total - limit), min(limit, total - 1) + 1)
        return jnp.stack([one, total - one])
    sizes = jnp.asarray(length_profile(number_of, total, limit, lean), jnp.int32)
    couples = (number_of - 1) // 2
    source_of, taker = sizes[1:1 + 2 * couples:2], sizes[2:2 + 2 * couples:2]
    room = jnp.minimum(source_of - 1, limit - taker)
    moved = jax.random.randint(jax.random.fold_in(stream_key, 1), (couples,), 0, 1 << 20) % (room + 1)
    sizes = sizes.at[1:1 + 2 * couples:2].set(source_of - moved).at[2:2 + 2 * couples:2].set(taker + moved)
    return sizes[jax.random.permutation(jax.random.fold_in(stream_key, 2), number_of)]


def noise(stream_key, dims, spread, bound, split=(), kind=jnp.bfloat16):
    entries = jax.random.normal(stream_key, dims, jnp.float32) * spread
    if len(split) > 0:
        entries = block_levels(stream_key, dims, split, -0.22, 0.18) * entries
    return jnp.clip(entries, min=-bound, max=bound).astype(kind)


def setup_inputs(seed: int = 0) -> dict:
    keys = jax.random.split(jax.random.key(seed), 8)
    first_stream = noise(keys[0], (TOKENS, D), 1.0, 6.0, ((0, 256),))
    second_stream = noise(keys[1], (TOKENS, D), 1.0, 6.0, ((0, 256),))
    value_stream = noise(keys[2], (TOKENS, D), 1.0, 6.0, ((0, 256),))
    short_filter = noise(keys[3], (3, SHORT, GROUPS), SHORT ** -0.5, 2.0)
    long_filter = noise(keys[4], (LONG, GROUPS), LONG ** -0.5, 0.5)
    skip_gain = noise(keys[5], (D,), 0.5, 3.0, (), jnp.float32)
    lengths = ragged(keys[6], NSEG, TOKENS, SEG_MOST, 2).astype(jnp.int32)
    return {"first_stream": first_stream, "second_stream": second_stream, "value_stream": value_stream, "short_filter": short_filter, "long_filter": long_filter, "skip_gain": skip_gain, "lengths": lengths}


def offsets_in_segment(lengths, row_count):
    ends = jnp.cumsum(lengths).astype(jnp.int32)
    starts = ends - lengths
    positions = jnp.arange(row_count, dtype=jnp.int32)
    inside = starts[None, :] <= positions[:, None]
    begins = jnp.max(jnp.where(inside, starts[None, :], jnp.zeros_like(starts)[None, :]), axis=1)
    return positions - begins


def reference(first_stream, second_stream, value_stream, short_filter, long_filter, skip_gain, lengths):
    pad_rows = LONG - 1 + SHORT - 1
    window_len = 2 * LONG - 1
    offsets = offsets_in_segment(lengths, TOKENS)
    offsets_padded = jnp.concatenate([jnp.full((pad_rows,), -1, jnp.int32), offsets])
    padded = [jnp.concatenate([jnp.zeros((pad_rows, D), jnp.bfloat16), stream], axis=0)
              for stream in (first_stream, second_stream, value_stream)]
    short_taps = jnp.repeat(short_filter.astype(jnp.float32), GROUP, axis=2)
    lag_table = (jnp.arange(LONG, dtype=jnp.int32)[:, None] + (LONG - 1)
                 - jnp.arange(window_len, dtype=jnp.int32)[None, :])
    in_range = (lag_table >= 0) & (lag_table < LONG)
    toeplitz = jnp.where(in_range[:, :, None],
                         long_filter.astype(jnp.float32)[jnp.clip(lag_table, 0, LONG - 1)], 0.0)

    def one_block(block_index):
        start = block_index * LONG
        window_rows = [lax.dynamic_slice_in_dim(stream, start, window_len + SHORT - 1, 0) for stream in padded]
        window_offsets = lax.dynamic_slice_in_dim(offsets_padded, start + SHORT - 1, window_len, 0)
        features = []
        for which in range(3):
            summed = jnp.zeros((window_len, D), jnp.float32)
            for tap_index in range(SHORT):
                shifted = window_rows[which][SHORT - 1 - tap_index: SHORT - 1 - tap_index + window_len].astype(jnp.float32)
                summed = summed + jnp.where((tap_index <= window_offsets)[:, None],
                                            short_taps[which, tap_index][None, :] * shifted, 0.0)
            features.append(summed)
        mixed_in = (features[0] * features[2]).astype(jnp.bfloat16)
        gate = features[1][LONG - 1:].astype(jnp.bfloat16)
        own_offsets = window_offsets[LONG - 1:]
        keep_mask = lag_table <= own_offsets[:, None]
        weights = jnp.where(keep_mask[:, :, None], toeplitz, 0.0)
        convolved = jnp.einsum("tsg,sgc->tgc", weights,
                               mixed_in.astype(jnp.float32).reshape(window_len, GROUPS, GROUP),
                               precision=lax.Precision.HIGHEST).reshape(LONG, D)
        own_mixed = mixed_in[LONG - 1:].astype(jnp.float32)
        gated = gate.astype(jnp.float32) * (convolved + skip_gain[None, :] * own_mixed)
        return gated.astype(jnp.bfloat16)

    blocks = lax.map(one_block, jnp.arange(TOKENS // LONG, dtype=jnp.int32))
    return blocks.reshape(TOKENS, D).T
```

```python
import functools

import jax
import jax.numpy as jnp
from jax import lax
from jax.experimental import pallas as pl
from jax.experimental.pallas import tpu as pltpu
from jax.sharding import PartitionSpec as P

MESH = pl.DeviceIdType.MESH
CTX = 64
TP = 4
NDEV = CTX * TP
ROWS = 128
LANES = 128
CH = 32
TILES = 64
SHORT = 7
HALO = 8
STRIDE = 43
HALO_LAG = 3
PER_CHUNK = 4
CHUNKS = TILES // PER_CHUNK
LAG = 3
F32 = jnp.float32
BF16 = jnp.bfloat16


def starts_of(lengths_ref, positions):
    begin = jnp.zeros_like(positions)
    start = jnp.int32(0)
    for j in range(15):
        start = start + lengths_ref[j]
        begin = jnp.where(positions >= start, start, begin)
    return begin


def segment_start(lengths_ref, position):
    begin = jnp.int32(0)
    start = jnp.int32(0)
    for j in range(15):
        start = start + lengths_ref[j]
        begin = jnp.where(position >= start, start, begin)
    return begin


def iota(shape, dim):
    return lax.broadcasted_iota(jnp.int32, shape, dim)


def nt_dot(a, b):
    return lax.dot_general(a, b, (((1,), (1,)), ((), ())), preferred_element_type=F32)


def kernel(
    lengths_ref, first_hbm, second_hbm, value_hbm, short_ref, long_ref, skip_ref, out_ref,
    streams, raw_halo, padded, taps, keep, long_rows, own_mask, prev_mask, head_mask,
    send_buf, recv_buf, halo_buf, out_buf, ident,
    load_sem, raw_send, raw_recv, one_send, one_recv, own_sem, halo_send, halo_recv, two_send, two_recv,
):
    ctx = lax.axis_index("ctx")
    tp = lax.axis_index("tp")
    me = ctx * TP + tp
    after = lax.rem(me + 1, NDEV)
    before = lax.rem(me + NDEV - 1, NDEV)
    after_ctx, after_tp = after // TP, lax.rem(after, TP)
    sources = (first_hbm, second_hbm, value_hbm)

    barrier = pltpu.get_barrier_semaphore()

    def greet(i, carry):
        pl.semaphore_signal(
            barrier, inc=1, device_id=(lax.rem(ctx + i, CTX), tp), device_id_type=MESH
        )
        return carry

    for d in range(1, TP):
        pl.semaphore_signal(
            barrier, inc=1, device_id=(ctx, lax.rem(tp + d, TP)), device_id_type=MESH
        )
    for other in (after, before):
        pl.semaphore_signal(
            barrier, inc=1, device_id=(other // TP, lax.rem(other, TP)), device_id_type=MESH
        )
    lax.fori_loop(1, CTX, greet, 0)

    loads = [
        pltpu.make_async_copy(sources[s], streams.at[s], load_sem.at[s]) for s in range(3)
    ]
    for load in loads:
        load.start()

    spread = (iota((LANES, 2048), 1) // 16 == iota((LANES, 2048), 0)).astype(BF16)
    for s in range(3):
        for q in range(4):
            wide = jnp.dot(
                short_ref[s, :, q * LANES : (q + 1) * LANES], spread, preferred_element_type=F32
            )
            for j in range(16):
                taps[q * 16 + j, s, 0:SHORT, :] = wide[:, j * LANES : (j + 1) * LANES]
    eye = (iota((LANES, LANES), 0) == iota((LANES, LANES), 1)).astype(BF16)
    ident[...] = eye
    for q in range(4):
        long_rows[q * LANES : (q + 1) * LANES, :] = nt_dot(
            eye, long_ref[:, q * LANES : (q + 1) * LANES]
        )
    place = me * ROWS + iota((ROWS, LANES), 0)
    offset = place - starts_of(lengths_ref, place)
    for k in range(1, SHORT):
        keep[k] = jnp.where(offset >= k, 1.0, 0.0)
    for b in range(4):
        base = ctx * 512 + b * ROWS
        at = base + iota((LANES, LANES), 1)
        begin = starts_of(lengths_ref, at)
        src = base + iota((LANES, LANES), 0)
        own_mask[b] = jnp.where((src >= begin) & (src <= at), 1.0, 0.0).astype(BF16)
        head = segment_start(lengths_ref, base)
        prev_at = base - ROWS + iota((CH, LANES), 1)
        prev_mask[b] = jnp.where(prev_at >= head, 1.0, 0.0).astype(BF16)
        row_at = base + iota((CH, LANES), 1)
        head_mask[b] = jnp.where(starts_of(lengths_ref, row_at) <= base, 1.0, 0.0)

    pl.semaphore_wait(barrier, CTX - 1 + TP - 1 + 2)

    def send_raw(k):
        def one(j, carry):
            i = k * PER_CHUNK + j
            tile = lax.rem(after_ctx + STRIDE * i, CTX)
            for s in range(3):
                pltpu.make_async_remote_copy(
                    sources[s].at[pl.ds(ROWS - HALO, HALO), pl.ds(pl.multiple_of(tile * LANES, LANES), LANES)],
                    raw_halo.at[i, s],
                    raw_send,
                    raw_recv.at[k],
                    device_id=(after_ctx, after_tp),
                    device_id_type=MESH,
                ).start()
            return carry

        lax.fori_loop(0, PER_CHUNK, one, 0)

    def short_chunk(k):
        here = raw_halo.at[pl.ds(k * PER_CHUNK, PER_CHUNK)]
        pltpu.make_async_copy(here, here, raw_recv.at[k]).wait()

        def one(j, carry):
            i = k * PER_CHUNK + j
            tile = lax.rem(ctx + STRIDE * i, CTX)
            lanes = pl.ds(pl.multiple_of(tile * LANES, LANES), LANES)
            features = []
            for s in range(3):
                padded[s, 0:HALO, :] = raw_halo[i, s].astype(F32)
                padded[s, HALO:, :] = streams[s, :, lanes].astype(F32)
            for s in range(3):
                total = padded[s, HALO:, :] * taps[tile, s, 0:1, :]
                for t in range(1, SHORT):
                    total += (padded[s, HALO - t : HALO - t + ROWS, :] * keep[t]) * taps[tile, s, t : t + 1, :]
                features.append(total)
            mixed_in = (features[0] * features[2]).astype(BF16)
            gate = features[1].astype(BF16)
            unit = ident[...]
            send_buf[i, :, 0] = nt_dot(unit, mixed_in).astype(BF16).reshape(TP, CH, LANES)
            send_buf[i, :, 1] = nt_dot(unit, gate).astype(BF16).reshape(TP, CH, LANES)
            return carry

        lax.fori_loop(0, PER_CHUNK, one, 0)
        part = pl.ds(k * PER_CHUNK, PER_CHUNK)
        for d in range(1, TP):
            to = lax.rem(tp + d, TP)
            pltpu.make_async_remote_copy(
                send_buf.at[part, to],
                recv_buf.at[tp, part],
                one_send,
                one_recv.at[k],
                device_id=(ctx, to),
                device_id_type=MESH,
            ).start()
        pltpu.make_async_copy(send_buf.at[part, tp], recv_buf.at[tp, part], own_sem.at[k]).start()

    def forward_chunk(k):
        part = pl.ds(k * PER_CHUNK, PER_CHUNK)
        three = recv_buf.at[pl.ds(0, 3), part]
        pltpu.make_async_copy(three, three, one_recv.at[k]).wait()
        one_part = recv_buf.at[0, part]
        pltpu.make_async_copy(one_part, one_part, own_sem.at[k]).wait()

        def one(j, carry):
            i = k * PER_CHUNK + j
            slot = lax.rem(i + TILES - HALO_LAG, TILES)
            pltpu.make_async_remote_copy(
                recv_buf.at[3, i, 0],
                halo_buf.at[slot],
                halo_send,
                halo_recv.at[slot],
                device_id=(lax.rem(ctx + 1, CTX), tp),
                device_id_type=MESH,
            ).start()
            return carry

        lax.fori_loop(0, PER_CHUNK, one, 0)

    lower = (iota((LANES, LANES), 0) > iota((LANES, LANES), 1)).astype(BF16)

    def circulant(row):
        base = jnp.broadcast_to(row, (8, LANES))
        sub = iota((8, LANES), 0)
        for bit in (1, 2, 4):
            base = jnp.where((sub & bit) != 0, pltpu.roll(base, bit, 1), base)
        return jnp.concatenate(
            [base] + [pltpu.roll(base, 8 * q, 1) for q in range(1, 16)], axis=0
        ).astype(BF16)

    def pick(wide):
        parts = []
        for r in range(wide.shape[0] // CH):
            parts.append(wide[r * CH : r * CH + 16, :LANES])
            parts.append(wide[r * CH + 16 : (r + 1) * CH, LANES:])
        return jnp.concatenate(parts, axis=0)

    def long_chunk(k):
        def one(j, carry):
            i = k * PER_CHUNK + j
            tile = lax.rem(ctx + STRIDE * i, CTX)
            pltpu.make_async_copy(halo_buf.at[i], halo_buf.at[i], halo_recv.at[i]).wait()
            group = (tile * TP + tp) * 2
            both = [circulant(long_rows[pl.ds(group + g, 1), :]) for g in range(2)]
            gain_row = jnp.broadcast_to(skip_ref[pl.ds(tile, 1), :], (CH, LANES))
            at = iota((CH, LANES), 1) == tp * CH + iota((CH, LANES), 0)
            gain = jnp.sum(jnp.where(at, gain_row, 0.0), axis=1, keepdims=True)
            blocks = [recv_buf[b, i, 0] for b in range(4)]
            earlier = [halo_buf[i]] + blocks[:3]
            masked = jnp.concatenate([earlier[b] * prev_mask[b] for b in range(4)], axis=0)
            weights = jnp.concatenate([both[0] * lower, both[1] * lower], axis=1)
            prev = pick(jnp.dot(masked, weights, preferred_element_type=F32))
            for b in range(4):
                weights = jnp.concatenate([both[0] * own_mask[b], both[1] * own_mask[b]], axis=1)
                total = pick(jnp.dot(blocks[b], weights, preferred_element_type=F32))
                total += prev[b * CH : (b + 1) * CH] * head_mask[b]
                total += gain * blocks[b].astype(F32)
                out_buf[i, :, b * LANES : (b + 1) * LANES] = (
                    recv_buf[b, i, 1].astype(F32) * total
                ).astype(BF16)
            place_at = pl.ds(pl.multiple_of(ctx * 512, 512), 512)

            @pl.when(i > 0)
            def _():
                pltpu.make_async_remote_copy(
                    out_buf.at[i],
                    out_ref.at[:, place_at],
                    two_send,
                    two_recv,
                    device_id=(tile, tp),
                    device_id_type=MESH,
                ).start()

            @pl.when(i == 0)
            def _():
                pltpu.make_async_copy(out_buf.at[0], out_ref.at[:, place_at], load_sem.at[0]).start()

            return carry

        lax.fori_loop(0, PER_CHUNK, one, 0)

    send_raw(0)
    for load in loads:
        load.wait()

    def step(n, carry):
        @pl.when(n + 1 < CHUNKS)
        def _():
            send_raw(n + 1)

        @pl.when(n < CHUNKS)
        def _():
            short_chunk(n)

        @pl.when((n >= 1) & (n <= CHUNKS))
        def _():
            forward_chunk(n - 1)

        @pl.when(n >= LAG)
        def _():
            long_chunk(n - LAG)

        return carry

    lax.fori_loop(0, CHUNKS + LAG, step, 0)

    pltpu.make_async_copy(raw_halo, raw_halo, raw_send).wait()
    pltpu.make_async_copy(send_buf.at[:, pl.ds(0, 3)], send_buf.at[:, pl.ds(0, 3)], one_send).wait()
    pltpu.make_async_copy(halo_buf, halo_buf, halo_send).wait()
    rest = out_buf.at[pl.ds(0, TILES - 1)]
    pltpu.make_async_copy(rest, rest, two_send).wait()
    pltpu.make_async_copy(out_buf.at[0], out_buf.at[0], load_sem.at[0]).wait()
    pltpu.make_async_copy(rest, rest, two_recv).wait()


def on_device(
    first_stream, second_stream, value_stream, short_filter, long_filter, skip_gain, lengths
):
    any_spec = pl.BlockSpec(memory_space=pl.ANY)
    vmem = pl.BlockSpec(memory_space=pltpu.VMEM)
    dma = pltpu.SemaphoreType.DMA
    return pl.pallas_call(
        kernel,
        out_shape=jax.ShapeDtypeStruct((CH, 32768), BF16),
        in_specs=[pl.BlockSpec(memory_space=pltpu.SMEM), any_spec, any_spec, any_spec, vmem, vmem, vmem],
        out_specs=any_spec,
        scratch_shapes=[
            pltpu.VMEM((3, ROWS, 8192), BF16),
            pltpu.VMEM((TILES, 3, HALO, LANES), BF16),
            pltpu.VMEM((3, HALO + ROWS, LANES), F32),
            pltpu.VMEM((TILES, 3, 8, LANES), F32),
            pltpu.VMEM((SHORT, ROWS, LANES), F32),
            pltpu.VMEM((512, LANES), F32),
            pltpu.VMEM((4, LANES, LANES), BF16),
            pltpu.VMEM((4, CH, LANES), BF16),
            pltpu.VMEM((4, CH, LANES), F32),
            pltpu.VMEM((TILES, TP, 2, CH, LANES), BF16),
            pltpu.VMEM((TP, TILES, 2, CH, LANES), BF16),
            pltpu.VMEM((TILES, CH, LANES), BF16),
            pltpu.VMEM((TILES, CH, 512), BF16),
            pltpu.VMEM((LANES, LANES), BF16),
            dma((3,)),
            dma,
            dma((CHUNKS,)),
            dma,
            dma((CHUNKS,)),
            dma((CHUNKS,)),
            dma,
            dma((TILES,)),
            dma,
            dma,
        ],
        compiler_params=pltpu.CompilerParams(
            collective_id=0, has_side_effects=True, vmem_limit_bytes=60 << 20
        ),
    )(lengths, first_stream, second_stream, value_stream, short_filter, long_filter, skip_gain.reshape(64, 128))


def solution(mesh):
    tokens = P(("ctx", "tp"), None)
    return jax.shard_map(
        on_device,
        mesh=mesh,
        in_specs=(tokens, tokens, tokens, P(), P(), P(), P()),
        out_specs=tokens,
        check_vma=False,
    )
```

```python
import functools

import jax
import jax.numpy as jnp
from jax import lax
from jax.experimental import pallas as pl
from jax.experimental.pallas import tpu as pltpu
from jax.sharding import PartitionSpec as P

MESH = pl.DeviceIdType.MESH
CTX = 64
TP = 4
NDEV = CTX * TP
ROWS = 128
LANES = 128
CH = 32
TILES = 64
SHORT = 7
HALO = 8
STRIDE = 43
HALO_LAG = 3
PER_CHUNK = 4
CHUNKS = TILES // PER_CHUNK
LAG = 6
AHEAD = 4
FWD = 2
UNROLL = 2
REACH = (1, 2, 4, 8, 16)
F32 = jnp.float32
BF16 = jnp.bfloat16


def starts_of(lengths_ref, positions):
    begin = jnp.zeros_like(positions)
    start = jnp.int32(0)
    for j in range(15):
        start = start + lengths_ref[j]
        begin = jnp.where(positions >= start, start, begin)
    return begin


def segment_start(lengths_ref, position):
    begin = jnp.int32(0)
    start = jnp.int32(0)
    for j in range(15):
        start = start + lengths_ref[j]
        begin = jnp.where(position >= start, start, begin)
    return begin


def iota(shape, dim):
    return lax.broadcasted_iota(jnp.int32, shape, dim)


def nt_dot(a, b):
    return lax.dot_general(a, b, (((1,), (1,)), ((), ())), preferred_element_type=F32)


def kernel(
    lengths_ref, first_hbm, second_hbm, value_hbm, short_hbm, long_hbm, skip_hbm, out_ref,
    short_ref, long_ref, skip_ref,
    streams, raw_halo, padded, taps, keep, long_rows, own_mask, prev_mask, head_mask,
    send_buf, recv_buf, halo_buf, out_buf, ident, early, partial,
    load_sem, raw_send, raw_recv, one_send, one_recv, own_sem, halo_send, halo_recv, two_send, two_recv, met,
):
    ctx = lax.axis_index("ctx")
    tp = lax.axis_index("tp")
    me = ctx * TP + tp
    after = lax.rem(me + 1, NDEV)
    before = lax.rem(me + NDEV - 1, NDEV)
    after_ctx, after_tp = after // TP, lax.rem(after, TP)
    sources = (first_hbm, second_hbm, value_hbm)

    barrier = pltpu.get_barrier_semaphore()

    for d in range(1, TP):
        pl.semaphore_signal(
            barrier, inc=1, device_id=(ctx, lax.rem(tp + d, TP)), device_id_type=MESH
        )
    for other in (after, before):
        pl.semaphore_signal(
            barrier, inc=1, device_id=(other // TP, lax.rem(other, TP)), device_id_type=MESH
        )
    for d in (1, CTX - 1):
        pl.semaphore_signal(
            barrier, inc=1, device_id=(lax.rem(ctx + d, CTX), tp), device_id_type=MESH
        )

    loads = [
        pltpu.make_async_copy(sources[s], streams.at[s], load_sem.at[s]) for s in range(3)
    ]
    small = [
        pltpu.make_async_copy(src, dst, load_sem.at[3 + j])
        for j, (src, dst) in enumerate(
            ((short_hbm, short_ref), (long_hbm, long_ref), (skip_hbm, skip_ref))
        )
    ]
    for load in small + loads:
        load.start()
    for load in small:
        load.wait()

    spread = (iota((LANES, 2048), 1) // 16 == iota((LANES, 2048), 0)).astype(BF16)
    for s in range(3):
        for q in range(4):
            wide = jnp.dot(
                short_ref[s, :, q * LANES : (q + 1) * LANES], spread, preferred_element_type=F32
            )
            for j in range(16):
                taps[q * 16 + j, s, 0:SHORT, :] = wide[:, j * LANES : (j + 1) * LANES]
    eye = (iota((LANES, LANES), 0) == iota((LANES, LANES), 1)).astype(BF16)
    ident[...] = eye
    for q in range(4):
        long_rows[q * LANES : (q + 1) * LANES, :] = nt_dot(
            eye, long_ref[:, q * LANES : (q + 1) * LANES]
        )
    place = me * ROWS + iota((ROWS, LANES), 0)
    offset = place - starts_of(lengths_ref, place)
    for k in range(1, SHORT):
        keep[k] = jnp.where(offset >= k, 1.0, 0.0)
    for b in range(4):
        base = ctx * 512 + b * ROWS
        at = base + iota((LANES, LANES), 1)
        begin = starts_of(lengths_ref, at)
        src = base + iota((LANES, LANES), 0)
        own_mask[b] = jnp.where((src >= begin) & (src <= at), 1.0, 0.0).astype(BF16)
        head = segment_start(lengths_ref, base)
        prev_at = base - ROWS + iota((CH, LANES), 1)
        prev_mask[b] = jnp.where(prev_at >= head, 1.0, 0.0).astype(BF16)
        row_at = base + iota((CH, LANES), 1)
        head_mask[b] = jnp.where(starts_of(lengths_ref, row_at) <= base, 1.0, 0.0)

    pl.semaphore_wait(barrier, 2 + TP - 1 + 2)

    def reach(j):
        for d in (REACH[j], CTX - REACH[j]):
            pl.semaphore_signal(
                met.at[j], inc=1, device_id=(lax.rem(ctx + d, CTX), tp), device_id_type=MESH
            )

    def met_all(j):
        pl.semaphore_wait(met.at[j], 2)

    reach(0)

    def send_raw(k):
        def one(j, carry):
            i = k * PER_CHUNK + j
            tile = lax.rem(after_ctx + STRIDE * i, CTX)
            for s in range(3):
                pltpu.make_async_remote_copy(
                    sources[s].at[pl.ds(ROWS - HALO, HALO), pl.ds(pl.multiple_of(tile * LANES, LANES), LANES)],
                    raw_halo.at[i, s],
                    raw_send,
                    raw_recv.at[k],
                    device_id=(after_ctx, after_tp),
                    device_id_type=MESH,
                ).start()
            return carry

        lax.fori_loop(0, PER_CHUNK, one, 0)

    def short_chunk(k):
        here = raw_halo.at[pl.ds(k * PER_CHUNK, PER_CHUNK)]
        pltpu.make_async_copy(here, here, raw_recv.at[k]).wait()

        def one(i, u):
            tile = lax.rem(ctx + STRIDE * i, CTX)
            lanes = pl.ds(pl.multiple_of(tile * LANES, LANES), LANES)
            features = []
            for s in range(3):
                padded[u, s, 0:HALO, :] = raw_halo[i, s].astype(F32)
                padded[u, s, HALO:, :] = streams[s, :, lanes].astype(F32)
            for s in range(3):
                total = padded[u, s, HALO:, :] * taps[tile, s, 0:1, :]
                for t in range(1, SHORT):
                    total += (padded[u, s, HALO - t : HALO - t + ROWS, :] * keep[t]) * taps[tile, s, t : t + 1, :]
                features.append(total)
            mixed_in = (features[0] * features[2]).astype(BF16)
            gate = features[1].astype(BF16)
            unit = ident[...]
            turned = nt_dot(unit, jnp.concatenate([mixed_in, gate], axis=0)).astype(BF16)
            send_buf[i, :, 0] = turned[:, :LANES].reshape(TP, CH, LANES)
            send_buf[i, :, 1] = turned[:, LANES:].reshape(TP, CH, LANES)

        def some(j, carry):
            for u in range(UNROLL):
                one(k * PER_CHUNK + j * UNROLL + u, u)
            return carry

        lax.fori_loop(0, PER_CHUNK // UNROLL, some, 0)
        part = pl.ds(k * PER_CHUNK, PER_CHUNK)
        for d in range(1, TP):
            to = lax.rem(tp + d, TP)
            pltpu.make_async_remote_copy(
                send_buf.at[part, to],
                recv_buf.at[tp, part],
                one_send,
                one_recv.at[k],
                device_id=(ctx, to),
                device_id_type=MESH,
            ).start()
        pltpu.make_async_copy(send_buf.at[part, tp], recv_buf.at[tp, part], own_sem.at[k]).start()

    def forward_chunk(k):
        part = pl.ds(k * PER_CHUNK, PER_CHUNK)
        three = recv_buf.at[pl.ds(0, 3), part]
        pltpu.make_async_copy(three, three, one_recv.at[k]).wait()
        one_part = recv_buf.at[0, part]
        pltpu.make_async_copy(one_part, one_part, own_sem.at[k]).wait()

        def one(j, carry):
            i = k * PER_CHUNK + j
            slot = lax.rem(i + TILES - HALO_LAG, TILES)
            pltpu.make_async_remote_copy(
                recv_buf.at[3, i, 0],
                halo_buf.at[slot],
                halo_send,
                halo_recv.at[slot],
                device_id=(lax.rem(ctx + 1, CTX), tp),
                device_id_type=MESH,
            ).start()
            return carry

        lax.fori_loop(0, PER_CHUNK, one, 0)

    lower = (iota((LANES, LANES), 0) > iota((LANES, LANES), 1)).astype(BF16)

    def circulant(row):
        base = jnp.broadcast_to(row, (8, LANES))
        sub = iota((8, LANES), 0)
        for bit in (1, 2, 4):
            base = jnp.where((sub & bit) != 0, pltpu.roll(base, bit, 1), base)
        return jnp.concatenate(
            [base] + [pltpu.roll(base, 8 * q, 1) for q in range(1, 16)], axis=0
        ).astype(BF16)

    def pick(wide):
        parts = []
        for r in range(wide.shape[0] // CH):
            parts.append(wide[r * CH : r * CH + 16, :LANES])
            parts.append(wide[r * CH + 16 : (r + 1) * CH, LANES:])
        return jnp.concatenate(parts, axis=0)

    def ship(i, lo, width, sem):
        tile = lax.rem(ctx + STRIDE * i, CTX)
        to = pl.ds(pl.multiple_of(ctx * 512 + lo, LANES), width)
        part = out_buf.at[i, :, pl.ds(lo, width)]

        @pl.when(i > 0)
        def _():
            pltpu.make_async_remote_copy(
                part,
                out_ref.at[:, to],
                two_send,
                two_recv,
                device_id=(tile, tp),
                device_id_type=MESH,
            ).start()

        @pl.when(i == 0)
        def _():
            pltpu.make_async_copy(part, out_ref.at[:, to], load_sem.at[sem]).start()

    def main_tile(i):
        tile = lax.rem(ctx + STRIDE * i, CTX)
        group = (tile * TP + tp) * 2
        both = [circulant(long_rows[pl.ds(group + g, 1), :]) for g in range(2)]
        gain_row = jnp.broadcast_to(skip_ref[pl.ds(tile, 1), :], (CH, LANES))
        at = iota((CH, LANES), 1) == tp * CH + iota((CH, LANES), 0)
        gain = jnp.sum(jnp.where(at, gain_row, 0.0), axis=1, keepdims=True)
        blocks = [recv_buf[b, i, 0] for b in range(4)]
        masked = jnp.concatenate([blocks[b - 1] * prev_mask[b] for b in range(1, 4)], axis=0)
        weights = jnp.concatenate([both[0] * lower, both[1] * lower], axis=1)
        early[i] = weights
        prev = pick(jnp.dot(masked, weights, preferred_element_type=F32))
        for b in range(4):
            weights = jnp.concatenate([both[0] * own_mask[b], both[1] * own_mask[b]], axis=1)
            total = pick(jnp.dot(blocks[b], weights, preferred_element_type=F32))
            total += gain * blocks[b].astype(F32)
            if b == 0:
                partial[i] = total
            else:
                total += prev[(b - 1) * CH : b * CH] * head_mask[b]
                out_buf[i, :, b * LANES : (b + 1) * LANES] = (
                    recv_buf[b, i, 1].astype(F32) * total
                ).astype(BF16)

    def head_tile(i):
        prev = pick(jnp.dot(halo_buf[i] * prev_mask[0], early[i], preferred_element_type=F32))
        total = partial[i] + prev * head_mask[0]
        out_buf[i, :, 0:LANES] = (recv_buf[0, i, 1].astype(F32) * total).astype(BF16)

    def main_chunk(k):
        def some(j, carry):
            first = k * PER_CHUNK + j * UNROLL
            for u in range(UNROLL):
                main_tile(first + u)
            for u in range(UNROLL):
                ship(first + u, LANES, 3 * LANES, 0)
            return carry

        lax.fori_loop(0, PER_CHUNK // UNROLL, some, 0)

    def head_chunk(k):
        def some(j, carry):
            first = k * PER_CHUNK + j * UNROLL
            for u in range(UNROLL):
                here = halo_buf.at[first + u]
                pltpu.make_async_copy(here, here, halo_recv.at[first + u]).wait()
            for u in range(UNROLL):
                head_tile(first + u)
            for u in range(UNROLL):
                ship(first + u, 0, LANES, 1)
            return carry

        lax.fori_loop(0, PER_CHUNK // UNROLL, some, 0)

    for k in range(AHEAD):
        send_raw(k)
    for load in loads:
        load.wait()

    def step(n, carry):
        @pl.when(n + AHEAD < CHUNKS)
        def _():
            send_raw(n + AHEAD)

        @pl.when(n < CHUNKS)
        def _():
            short_chunk(n)

        for j in range(len(REACH)):

            @pl.when(n == (j + 1) // 2)
            def _():
                met_all(j)
                if j + 1 < len(REACH):
                    reach(j + 1)

        @pl.when((n >= FWD) & (n < CHUNKS + FWD))
        def _():
            forward_chunk(n - FWD)
            main_chunk(n - FWD)

        @pl.when(n >= LAG)
        def _():
            head_chunk(n - LAG)

        return carry

    lax.fori_loop(0, CHUNKS + LAG, step, 0)

    pltpu.make_async_copy(raw_halo, raw_halo, raw_send).wait()
    pltpu.make_async_copy(send_buf.at[:, pl.ds(0, 3)], send_buf.at[:, pl.ds(0, 3)], one_send).wait()
    pltpu.make_async_copy(halo_buf, halo_buf, halo_send).wait()
    rest = out_buf.at[pl.ds(0, TILES - 1)]
    pltpu.make_async_copy(rest, rest, two_send).wait()
    tail = out_buf.at[0, :, pl.ds(LANES, 3 * LANES)]
    pltpu.make_async_copy(tail, tail, load_sem.at[0]).wait()
    head = out_buf.at[0, :, pl.ds(0, LANES)]
    pltpu.make_async_copy(head, head, load_sem.at[1]).wait()
    pltpu.make_async_copy(rest, rest, two_recv).wait()


def on_device(
    first_stream, second_stream, value_stream, short_filter, long_filter, skip_gain, lengths
):
    any_spec = pl.BlockSpec(memory_space=pl.ANY)
    hbm = pl.BlockSpec(memory_space=pltpu.HBM)
    dma = pltpu.SemaphoreType.DMA
    return pl.pallas_call(
        kernel,
        out_shape=jax.ShapeDtypeStruct((CH, 32768), BF16),
        in_specs=[pl.BlockSpec(memory_space=pltpu.SMEM), hbm, hbm, hbm, hbm, hbm, hbm],
        out_specs=any_spec,
        scratch_shapes=[
            pltpu.VMEM((3, SHORT, 512), BF16),
            pltpu.VMEM((LANES, 512), BF16),
            pltpu.VMEM((64, LANES), F32),
            pltpu.VMEM((3, ROWS, 8192), BF16),
            pltpu.VMEM((TILES, 3, HALO, LANES), BF16),
            pltpu.VMEM((UNROLL, 3, HALO + ROWS, LANES), F32),
            pltpu.VMEM((TILES, 3, 8, LANES), F32),
            pltpu.VMEM((SHORT, ROWS, LANES), F32),
            pltpu.VMEM((512, LANES), F32),
            pltpu.VMEM((4, LANES, LANES), BF16),
            pltpu.VMEM((4, CH, LANES), BF16),
            pltpu.VMEM((4, CH, LANES), F32),
            pltpu.VMEM((TILES, TP, 2, CH, LANES), BF16),
            pltpu.VMEM((TP, TILES, 2, CH, LANES), BF16),
            pltpu.VMEM((TILES, CH, LANES), BF16),
            pltpu.VMEM((TILES, CH, 512), BF16),
            pltpu.VMEM((LANES, LANES), BF16),
            pltpu.VMEM((TILES, LANES, 2 * LANES), BF16),
            pltpu.VMEM((TILES, CH, LANES), F32),
            dma((6,)),
            dma,
            dma((CHUNKS,)),
            dma,
            dma((CHUNKS,)),
            dma((CHUNKS,)),
            dma,
            dma((TILES,)),
            dma,
            dma,
            pltpu.SemaphoreType.REGULAR((len(REACH),)),
        ],
        compiler_params=pltpu.CompilerParams(
            collective_id=0, has_side_effects=True, vmem_limit_bytes=50 << 20
        ),
    )(*(pltpu.with_memory_space_constraint(x, pltpu.HBM) for x in (lengths, first_stream, second_stream, value_stream, short_filter, long_filter, skip_gain.reshape(64, 128))))


def solution(mesh):
    tokens = P(("ctx", "tp"), None)
    return jax.shard_map(
        on_device,
        mesh=mesh,
        in_specs=(tokens, tokens, tokens, P(), P(), P(), P()),
        out_specs=tokens,
        check_vma=False,
    )
```

```python
import functools

import jax
import jax.numpy as jnp
from jax import lax
from jax.experimental import pallas as pl
from jax.experimental.pallas import tpu as pltpu
from jax.sharding import PartitionSpec as P

MESH = pl.DeviceIdType.MESH
CTX = 64
TP = 4
NDEV = CTX * TP
ROWS = 128
LANES = 128
CH = 32
TILES = 64
SHORT = 7
HALO = 8
STRIDE = 43
HALO_LAG = 3
PER_CHUNK = 4
CHUNKS = TILES // PER_CHUNK
LAG = 4
AHEAD = 3
FWD = 2
UNROLL = 2
REACH = (1, 2, 4, 8, 16)
F32 = jnp.float32
BF16 = jnp.bfloat16


def starts_of(lengths_ref, positions):
    begin = jnp.zeros_like(positions)
    start = jnp.int32(0)
    for j in range(15):
        start = start + lengths_ref[j]
        begin = jnp.where(positions >= start, start, begin)
    return begin


def segment_start(lengths_ref, position):
    begin = jnp.int32(0)
    start = jnp.int32(0)
    for j in range(15):
        start = start + lengths_ref[j]
        begin = jnp.where(position >= start, start, begin)
    return begin


def iota(shape, dim):
    return lax.broadcasted_iota(jnp.int32, shape, dim)


def nt_dot(a, b):
    return lax.dot_general(a, b, (((1,), (1,)), ((), ())), preferred_element_type=F32)


def kernel(
    lengths_ref, first_hbm, second_hbm, value_hbm, short_hbm, long_hbm, skip_hbm, out_ref,
    short_ref, long_ref, skip_ref,
    streams, raw_out, raw_halo, padded, taps, keep, long_rows, own_mask, prev_mask, head_mask,
    send_buf, recv_buf, halo_buf, out_buf, ident, early, partial,
    load_sem, raw_send, raw_recv, one_send, one_recv, own_sem, halo_send, halo_recv, two_send, two_recv, met,
):
    ctx = lax.axis_index("ctx")
    tp = lax.axis_index("tp")
    me = ctx * TP + tp
    after = lax.rem(me + 1, NDEV)
    before = lax.rem(me + NDEV - 1, NDEV)
    after_ctx, after_tp = after // TP, lax.rem(after, TP)
    sources = (first_hbm, second_hbm, value_hbm)

    barrier = pltpu.get_barrier_semaphore()

    for d in range(1, TP):
        pl.semaphore_signal(
            barrier, inc=1, device_id=(ctx, lax.rem(tp + d, TP)), device_id_type=MESH
        )
    for other in (after, before):
        pl.semaphore_signal(
            barrier, inc=1, device_id=(other // TP, lax.rem(other, TP)), device_id_type=MESH
        )
    for d in (1, CTX - 1):
        pl.semaphore_signal(
            barrier, inc=1, device_id=(lax.rem(ctx + d, CTX), tp), device_id_type=MESH
        )

    loads = [
        pltpu.make_async_copy(sources[s], streams.at[s], load_sem.at[s]) for s in range(3)
    ]
    small = [
        pltpu.make_async_copy(src, dst, load_sem.at[3 + j])
        for j, (src, dst) in enumerate(
            ((short_hbm, short_ref), (long_hbm, long_ref), (skip_hbm, skip_ref))
        )
    ]
    for load in small + loads:
        load.start()
    for load in small:
        load.wait()

    spread = (iota((LANES, 2048), 1) // 16 == iota((LANES, 2048), 0)).astype(BF16)
    for s in range(3):
        for q in range(4):
            wide = jnp.dot(
                short_ref[s, :, q * LANES : (q + 1) * LANES], spread, preferred_element_type=F32
            )
            for j in range(16):
                taps[q * 16 + j, s, 0:SHORT, :] = wide[:, j * LANES : (j + 1) * LANES]
    eye = (iota((LANES, LANES), 0) == iota((LANES, LANES), 1)).astype(BF16)
    ident[...] = eye
    for q in range(4):
        long_rows[q * LANES : (q + 1) * LANES, :] = nt_dot(
            eye, long_ref[:, q * LANES : (q + 1) * LANES]
        )
    place = me * ROWS + iota((ROWS, LANES), 0)
    offset = place - starts_of(lengths_ref, place)
    for k in range(1, SHORT):
        keep[k] = jnp.where(offset >= k, 1.0, 0.0)
    for b in range(4):
        base = ctx * 512 + b * ROWS
        at = base + iota((LANES, LANES), 1)
        begin = starts_of(lengths_ref, at)
        src = base + iota((LANES, LANES), 0)
        own_mask[b] = jnp.where((src >= begin) & (src <= at), 1.0, 0.0).astype(BF16)
        head = segment_start(lengths_ref, base)
        prev_at = base - ROWS + iota((CH, LANES), 1)
        prev_mask[b] = jnp.where(prev_at >= head, 1.0, 0.0).astype(BF16)
        row_at = base + iota((CH, LANES), 1)
        head_mask[b] = jnp.where(starts_of(lengths_ref, row_at) <= base, 1.0, 0.0)

    pl.semaphore_wait(barrier, 2 + TP - 1 + 2)

    def reach(j):
        for d in (REACH[j], CTX - REACH[j]):
            pl.semaphore_signal(
                met.at[j], inc=1, device_id=(lax.rem(ctx + d, CTX), tp), device_id_type=MESH
            )

    def met_all(j):
        pl.semaphore_wait(met.at[j], 2)

    reach(0)

    def send_raw(k):
        def one(j, carry):
            i = k * PER_CHUNK + j
            tile = lax.rem(after_ctx + STRIDE * i, CTX)
            lanes = pl.ds(pl.multiple_of(tile * LANES, LANES), LANES)
            for s in range(3):
                last = streams[s, ROWS - 16 : ROWS, lanes].astype(F32)
                for h in range(3):
                    raw_out[i, s, h] = last[10 + 2 * h : 12 + 2 * h].astype(BF16)
            return carry

        lax.fori_loop(0, PER_CHUNK, one, 0)
        part = pl.ds(k * PER_CHUNK, PER_CHUNK)
        pltpu.make_async_remote_copy(
            raw_out.at[part],
            raw_halo.at[part],
            raw_send,
            raw_recv.at[k],
            device_id=(after_ctx, after_tp),
            device_id_type=MESH,
        ).start()

    def short_chunk(k):
        here = raw_halo.at[pl.ds(k * PER_CHUNK, PER_CHUNK)]
        pltpu.make_async_copy(here, here, raw_recv.at[k]).wait()

        def one(i, u):
            tile = lax.rem(ctx + STRIDE * i, CTX)
            lanes = pl.ds(pl.multiple_of(tile * LANES, LANES), LANES)
            features = []
            for s in range(3):
                for h in range(3):
                    padded[u, s, 2 + 2 * h : 4 + 2 * h, :] = raw_halo[i, s, h].astype(F32)
                padded[u, s, HALO:, :] = streams[s, :, lanes].astype(F32)
            for s in range(3):
                total = padded[u, s, HALO:, :] * taps[tile, s, 0:1, :]
                for t in range(1, SHORT):
                    total += (padded[u, s, HALO - t : HALO - t + ROWS, :] * keep[t]) * taps[tile, s, t : t + 1, :]
                features.append(total)
            mixed_in = (features[0] * features[2]).astype(BF16)
            gate = features[1].astype(BF16)
            unit = ident[...]
            turned = nt_dot(unit, jnp.concatenate([mixed_in, gate], axis=0)).astype(BF16)
            send_buf[i, :, 0] = turned[:, :LANES].reshape(TP, CH, LANES)
            send_buf[i, :, 1] = turned[:, LANES:].reshape(TP, CH, LANES)

        def some(j, carry):
            for u in range(UNROLL):
                one(k * PER_CHUNK + j * UNROLL + u, u)
            return carry

        lax.fori_loop(0, PER_CHUNK // UNROLL, some, 0)
        part = pl.ds(k * PER_CHUNK, PER_CHUNK)
        for d in range(1, TP):
            to = lax.rem(tp + d, TP)
            pltpu.make_async_remote_copy(
                send_buf.at[part, to],
                recv_buf.at[tp, part],
                one_send,
                one_recv.at[k],
                device_id=(ctx, to),
                device_id_type=MESH,
            ).start()
        pltpu.make_async_copy(send_buf.at[part, tp], recv_buf.at[tp, part], own_sem.at[k]).start()

    def forward_chunk(k):
        part = pl.ds(k * PER_CHUNK, PER_CHUNK)
        three = recv_buf.at[pl.ds(0, 3), part]
        pltpu.make_async_copy(three, three, one_recv.at[k]).wait()
        one_part = recv_buf.at[0, part]
        pltpu.make_async_copy(one_part, one_part, own_sem.at[k]).wait()

        def one(j, carry):
            i = k * PER_CHUNK + j
            slot = lax.rem(i + TILES - HALO_LAG, TILES)
            pltpu.make_async_remote_copy(
                recv_buf.at[3, i, 0],
                halo_buf.at[slot],
                halo_send,
                halo_recv.at[slot],
                device_id=(lax.rem(ctx + 1, CTX), tp),
                device_id_type=MESH,
            ).start()
            return carry

        lax.fori_loop(0, PER_CHUNK, one, 0)

    lower = (iota((LANES, LANES), 0) > iota((LANES, LANES), 1)).astype(BF16)

    def circulant(row):
        base = jnp.broadcast_to(row, (8, LANES))
        sub = iota((8, LANES), 0)
        for bit in (1, 2, 4):
            base = jnp.where((sub & bit) != 0, pltpu.roll(base, bit, 1), base)
        return jnp.concatenate(
            [base] + [pltpu.roll(base, 8 * q, 1) for q in range(1, 16)], axis=0
        ).astype(BF16)

    def pick(wide):
        parts = []
        for r in range(wide.shape[0] // CH):
            parts.append(wide[r * CH : r * CH + 16, :LANES])
            parts.append(wide[r * CH + 16 : (r + 1) * CH, LANES:])
        return jnp.concatenate(parts, axis=0)

    def ship(i, lo, width, sem):
        tile = lax.rem(ctx + STRIDE * i, CTX)
        to = pl.ds(pl.multiple_of(ctx * 512 + lo, LANES), width)
        part = out_buf.at[i, :, pl.ds(lo, width)]

        @pl.when(i > 0)
        def _():
            pltpu.make_async_remote_copy(
                part,
                out_ref.at[:, to],
                two_send,
                two_recv,
                device_id=(tile, tp),
                device_id_type=MESH,
            ).start()

        @pl.when(i == 0)
        def _():
            pltpu.make_async_copy(part, out_ref.at[:, to], load_sem.at[sem]).start()

    def main_tile(i):
        tile = lax.rem(ctx + STRIDE * i, CTX)
        group = (tile * TP + tp) * 2
        both = [circulant(long_rows[pl.ds(group + g, 1), :]) for g in range(2)]
        gain_row = jnp.broadcast_to(skip_ref[pl.ds(tile, 1), :], (CH, LANES))
        at = iota((CH, LANES), 1) == tp * CH + iota((CH, LANES), 0)
        gain = jnp.sum(jnp.where(at, gain_row, 0.0), axis=1, keepdims=True)
        blocks = [recv_buf[b, i, 0] for b in range(4)]
        masked = jnp.concatenate([blocks[b - 1] * prev_mask[b] for b in range(1, 4)], axis=0)
        weights = jnp.concatenate([both[0] * lower, both[1] * lower], axis=1)
        early[i] = weights
        prev = pick(jnp.dot(masked, weights, preferred_element_type=F32))
        for b in range(4):
            weights = jnp.concatenate([both[0] * own_mask[b], both[1] * own_mask[b]], axis=1)
            total = pick(jnp.dot(blocks[b], weights, preferred_element_type=F32))
            total += gain * blocks[b].astype(F32)
            if b == 0:
                partial[i] = total
            else:
                total += prev[(b - 1) * CH : b * CH] * head_mask[b]
                out_buf[i, :, b * LANES : (b + 1) * LANES] = (
                    recv_buf[b, i, 1].astype(F32) * total
                ).astype(BF16)

    def head_tile(i):
        prev = pick(jnp.dot(halo_buf[i] * prev_mask[0], early[i], preferred_element_type=F32))
        total = partial[i] + prev * head_mask[0]
        out_buf[i, :, 0:LANES] = (recv_buf[0, i, 1].astype(F32) * total).astype(BF16)

    def main_chunk(k):
        def some(j, carry):
            first = k * PER_CHUNK + j * UNROLL
            for u in range(UNROLL):
                main_tile(first + u)
            for u in range(UNROLL):
                ship(first + u, LANES, 3 * LANES, 0)
            return carry

        lax.fori_loop(0, PER_CHUNK // UNROLL, some, 0)

    def head_chunk(k):
        def some(j, carry):
            first = k * PER_CHUNK + j * UNROLL
            for u in range(UNROLL):
                here = halo_buf.at[first + u]
                pltpu.make_async_copy(here, here, halo_recv.at[first + u]).wait()
            for u in range(UNROLL):
                head_tile(first + u)
            for u in range(UNROLL):
                ship(first + u, 0, LANES, 1)
            return carry

        lax.fori_loop(0, PER_CHUNK // UNROLL, some, 0)

    for load in loads:
        load.wait()
    for k in range(AHEAD):
        send_raw(k)

    def step(n, carry):
        @pl.when(n + AHEAD < CHUNKS)
        def _():
            send_raw(n + AHEAD)

        @pl.when(n < CHUNKS)
        def _():
            short_chunk(n)

        for j in range(len(REACH)):

            @pl.when(n == (j + 1) // 2)
            def _():
                met_all(j)
                if j + 1 < len(REACH):
                    reach(j + 1)

        @pl.when((n >= FWD) & (n < CHUNKS + FWD))
        def _():
            forward_chunk(n - FWD)
            main_chunk(n - FWD)

        @pl.when(n >= LAG)
        def _():
            head_chunk(n - LAG)

        return carry

    lax.fori_loop(0, CHUNKS + LAG, step, 0)

    pltpu.make_async_copy(raw_halo, raw_halo, raw_send).wait()
    pltpu.make_async_copy(send_buf.at[:, pl.ds(0, 3)], send_buf.at[:, pl.ds(0, 3)], one_send).wait()
    pltpu.make_async_copy(halo_buf, halo_buf, halo_send).wait()
    rest = out_buf.at[pl.ds(0, TILES - 1)]
    pltpu.make_async_copy(rest, rest, two_send).wait()
    tail = out_buf.at[0, :, pl.ds(LANES, 3 * LANES)]
    pltpu.make_async_copy(tail, tail, load_sem.at[0]).wait()
    head = out_buf.at[0, :, pl.ds(0, LANES)]
    pltpu.make_async_copy(head, head, load_sem.at[1]).wait()
    pltpu.make_async_copy(rest, rest, two_recv).wait()


def on_device(
    first_stream, second_stream, value_stream, short_filter, long_filter, skip_gain, lengths
):
    any_spec = pl.BlockSpec(memory_space=pl.ANY)
    hbm = pl.BlockSpec(memory_space=pltpu.HBM)
    dma = pltpu.SemaphoreType.DMA
    return pl.pallas_call(
        kernel,
        out_shape=jax.ShapeDtypeStruct((CH, 32768), BF16),
        in_specs=[pl.BlockSpec(memory_space=pltpu.SMEM), hbm, hbm, hbm, hbm, hbm, hbm],
        out_specs=any_spec,
        scratch_shapes=[
            pltpu.VMEM((3, SHORT, 512), BF16),
            pltpu.VMEM((LANES, 512), BF16),
            pltpu.VMEM((64, LANES), F32),
            pltpu.VMEM((3, ROWS, 8192), BF16),
            pltpu.VMEM((TILES, 3, 3, 2, LANES), BF16),
            pltpu.VMEM((TILES, 3, 3, 2, LANES), BF16),
            pltpu.VMEM((UNROLL, 3, HALO + ROWS, LANES), F32),
            pltpu.VMEM((TILES, 3, 8, LANES), F32),
            pltpu.VMEM((SHORT, ROWS, LANES), F32),
            pltpu.VMEM((512, LANES), F32),
            pltpu.VMEM((4, LANES, LANES), BF16),
            pltpu.VMEM((4, CH, LANES), BF16),
            pltpu.VMEM((4, CH, LANES), F32),
            pltpu.VMEM((TILES, TP, 2, CH, LANES), BF16),
            pltpu.VMEM((TP, TILES, 2, CH, LANES), BF16),
            pltpu.VMEM((TILES, CH, LANES), BF16),
            pltpu.VMEM((TILES, CH, 512), BF16),
            pltpu.VMEM((LANES, LANES), BF16),
            pltpu.VMEM((TILES, LANES, 2 * LANES), BF16),
            pltpu.VMEM((TILES, CH, LANES), F32),
            dma((6,)),
            dma,
            dma((CHUNKS,)),
            dma,
            dma((CHUNKS,)),
            dma((CHUNKS,)),
            dma,
            dma((TILES,)),
            dma,
            dma,
            pltpu.SemaphoreType.REGULAR((len(REACH),)),
        ],
        compiler_params=pltpu.CompilerParams(
            collective_id=0, has_side_effects=True, vmem_limit_bytes=50 << 20
        ),
    )(*(pltpu.with_memory_space_constraint(x, pltpu.HBM) for x in (lengths, first_stream, second_stream, value_stream, short_filter, long_filter, skip_gain.reshape(64, 128))))


def solution(mesh):
    tokens = P(("ctx", "tp"), None)
    return jax.shard_map(
        on_device,
        mesh=mesh,
        in_specs=(tokens, tokens, tokens, P(), P(), P(), P()),
        out_specs=tokens,
        check_vma=False,
    )
```
